32 devices in a mesh: head: 4 (over y, x), ctx: 8 (over z, core).
Axes of the slice: x: 2, y: 2, z: 4, core: 2. Of those that a mesh axis runs over, the one named last changes fastest.
Arguments:
- queries: bfloat16 [3, 4096, 5120], P(None, 'ctx', 'head'), may hold values from -6 to 6
- keys: bfloat16 [3, 4096, 5120], P(None, 'ctx', 'head'), may hold values from -6 to 6
- values: bfloat16 [3, 4096, 5120], P(None, 'ctx', 'head'), may hold values from -6 to 6
- features: bfloat16 [3, 4096, 5120], P(None, 'ctx', 'head'), may hold values from -6 to 6
- w_rate: bfloat16 [5120, 60], P('head'), may hold values from -0.078125 to 0.078125
- fast_init: bfloat16 [20, 3, 256, 256], P('head'), may hold values from -0.375 to 0.375
- momentum: float32 [20], P('head'), may hold values from 0.3 to 0.95
Outputs:
- mixed: bfloat16 [3, 4096, 5120], P(None, 'ctx', 'head')
The draws below stay inside these ranges and needn't reach their ends.
All inputs are finite; a program needn't handle non-finite values.
Results may differ from the reference program's by a relative error of at most 0.014.
Values may be sent and summed in bfloat16 or wider, within the bound.
No kernel may reach another device: no remote copies, remote signals or barrier semaphores. Data moves between devices by JAX's collectives and lax.ppermute only.
A program may use at most 128 MiB of HBM per device.

```python
import jax
import jax.numpy as jnp
from jax import lax

DH = 256
HEADS = 20
GROUPS = 3
D = 5120
GROUP = 4096


def block_scale(own_key, shape, pieces, smallest, top_value):
    def one(position, parts):
        steps = jax.random.uniform(jax.random.fold_in(jax.random.fold_in(own_key, 6), position), (parts,), jnp.float32, smallest / len(pieces), top_value / len(pieces))
        return jnp.repeat(jnp.exp(steps), shape[position] // parts).reshape((-1,) + (1,) * (len(shape) - position - 1))

    loudness = one(*pieces[0])
    for cut in pieces[1:]:
        loudness = loudness * one(*cut)
    return loudness


def scatter_about(own_key, shape, width, limit, cuts=(), held_as=jnp.bfloat16):
    factor_of = block_scale(own_key, shape, cuts, -0.22, 0.18) if cuts else 1.0
    drawn = jax.random.normal(own_key, shape, jnp.float32) * width * factor_of
    return jnp.minimum(jnp.maximum(drawn, -limit), limit).astype(held_as)


def setup_inputs(seed: int = 0) -> dict:
    streams_of = jax.random.split(jax.random.key(seed), 8)
    queries = scatter_about(streams_of[0], (GROUPS, GROUP, D), 1.0, 6.0, ((1, 8), (2, 4)))
    keys = scatter_about(streams_of[1], (GROUPS, GROUP, D), 1.0, 6.0, ((1, 8), (2, 4)))
    values = scatter_about(streams_of[2], (GROUPS, GROUP, D), 1.0, 6.0, ((1, 8), (2, 4)))
    features = scatter_about(streams_of[3], (GROUPS, GROUP, D), 1.0, 6.0, ((1, 8), (2, 4)))
    w_rate = scatter_about(streams_of[4], (D, 3 * HEADS), D ** -0.5, 0.078125, ((0, 4),))
    fast_init = scatter_about(streams_of[5], (HEADS, 3, DH, DH), DH ** -0.5, 0.375, ((0, 4),))
    momentum = jnp.clip(0.3 + 0.65 * jax.random.uniform(streams_of[6], (HEADS,), jnp.float32) ** block_scale(streams_of[6], (HEADS,), ((0, 4),), -0.2, 0.2), 0.3, 0.95)
    return dict(queries=queries, keys=keys, values=values, features=features, w_rate=w_rate, fast_init=fast_init, momentum=momentum)


def rms_cast(block):
    wide = block.astype(jnp.float32)
    scale = lax.rsqrt(lax.optimization_barrier(jnp.mean(wide * wide, axis=-1, keepdims=True)) + 1e-06)
    return (wide * scale).astype(jnp.bfloat16)

def matmul(left, right):
    return jnp.dot(left.astype(jnp.float32), right.astype(jnp.float32), preferred_element_type=jnp.float32)

def renorm(matrix, base):
    length = jnp.sqrt(lax.optimization_barrier(jnp.sum(matrix * matrix, axis=-1)) + 1e-06)
    return matrix * (base / length)[..., None]

def head_run(item):
    query_all, key_all, value_all, rate_all, initial, factor = item
    weights = initial.astype(jnp.float32)
    base = jnp.sqrt(lax.optimization_barrier(jnp.sum(weights * weights, axis=-1)))
    velocity = jnp.zeros_like(weights)
    outputs = []
    for group in range(GROUPS):
        key_norm = rms_cast(key_all[group])
        value_now = value_all[group]
        rate_now = rate_all[group]
        narrow = weights.astype(jnp.bfloat16)
        gate = matmul(key_norm, narrow[0])
        upper = matmul(key_norm, narrow[1])
        active = jax.nn.silu(gate)
        hidden_key = (active * upper).astype(jnp.bfloat16)
        back = matmul(value_now, narrow[2].T)
        sig = jax.nn.sigmoid(gate)
        d_gate = back * upper * sig * (1.0 + gate * (1.0 - sig))
        d_up = back * active
        err_gate = (rate_now[:, 0:1] * d_gate).astype(jnp.bfloat16)
        err_up = (rate_now[:, 2:3] * d_up).astype(jnp.bfloat16)
        err_down = (rate_now[:, 1:2] * value_now.astype(jnp.float32)).astype(jnp.bfloat16)
        grads = jnp.stack([matmul(key_norm.T, err_gate), matmul(key_norm.T, err_up), matmul(hidden_key.T, err_down)])
        velocity = factor * velocity + grads
        weights = renorm(weights + velocity, base)
        narrow = weights.astype(jnp.bfloat16)
        query_norm = rms_cast(query_all[group])
        hidden_query = (jax.nn.silu(matmul(query_norm, narrow[0])) * matmul(query_norm, narrow[1])).astype(jnp.bfloat16)
        outputs.append(matmul(hidden_query, narrow[2]).astype(jnp.bfloat16))
    return jnp.stack(outputs)

def reference(queries, keys, values, features, w_rate, fast_init, momentum):
    logits = jnp.einsum('cnd,dr->cnr', features.astype(jnp.float32), w_rate.astype(jnp.float32))
    rates = (0.001 * jax.nn.sigmoid(logits)).reshape(GROUPS, GROUP, HEADS, 3)

    def split(array):
        return array.reshape(GROUPS, GROUP, HEADS, DH).transpose(2, 0, 1, 3)
    result = lax.map(head_run, (split(queries), split(keys), split(values), rates.transpose(2, 0, 1, 3), fast_init, momentum))
    return result.transpose(1, 2, 0, 3).reshape(GROUPS, GROUP, HEADS * DH)
```

```python
import functools

import jax
import jax.numpy as jnp
from jax import lax
from jax.experimental import pallas as pl
from jax.experimental.pallas import tpu as pltpu
from jax.sharding import PartitionSpec as P


BF16, F32 = jnp.bfloat16, jnp.float32
WHOLE = pl.BlockSpec(memory_space=pltpu.VMEM)
SCALAR = pl.BlockSpec(memory_space=pltpu.SMEM)
OUTSIDE = pl.BlockSpec(memory_space=pltpu.HBM)


def near(array):
    return pltpu.with_memory_space_constraint(array, pltpu.VMEM)


def params(mib):
    return pltpu.CompilerParams(vmem_limit_bytes=mib << 20)


def dot(left, right, left_dim, right_dim):
    return lax.dot_general(
        left, right, (((left_dim,), (right_dim,)), ((), ())), preferred_element_type=F32
    )


def rms_cast(block):
    wide = block.astype(F32)
    scale = lax.rsqrt(jnp.mean(wide * wide, axis=-1, keepdims=True) + 1e-06)
    return (wide * scale).astype(BF16)


def logits_kernel(parts, features, rate_ref, out_ref, buffer, sems):
    groups, rows, _ = features.shape
    each = rate_ref.shape[1] // parts

    def fetch(group):
        return pltpu.make_async_copy(features.at[group], buffer.at[group], sems.at[group])

    for group in range(groups):
        fetch(group).start()
    for group in range(groups):
        fetch(group).wait()
        turned = jnp.transpose(dot(buffer[group], rate_ref[...], 1, 0))
        for part in range(parts):
            out_ref[part, :each, group * rows : (group + 1) * rows] = turned[
                part * each : (part + 1) * each
            ]


def partial_logits(features, w_rate, parts):
    groups, rows, width = features.shape
    each = w_rate.shape[1] // parts
    return pl.pallas_call(
        functools.partial(logits_kernel, parts),
        in_specs=[OUTSIDE, WHOLE],
        out_specs=WHOLE,
        out_shape=pltpu.VMEM((parts, each, groups * rows), F32),
        scratch_shapes=[
            pltpu.VMEM((groups, rows, width), BF16),
            pltpu.SemaphoreType.DMA((groups,)),
        ],
        compiler_params=params(12),
        name="logits",
    )(features, w_rate)


def rates_kernel(*refs):
    parts, out_ref = refs[:-1], refs[-1]
    total = parts[0][...]
    for part in parts[1:]:
        total = total + part[...]
    out_ref[: total.shape[0]] = 0.001 * jax.nn.sigmoid(total)


def rates_of(pieces):
    each, tokens = pieces[0].shape
    padded = -(-each // 8) * 8
    return pl.pallas_call(
        rates_kernel,
        in_specs=[WHOLE] * len(pieces),
        out_specs=WHOLE,
        out_shape=pltpu.VMEM((padded, tokens), F32),
        compiler_params=params(4),
        name="rates",
    )(*[near(piece) for piece in pieces])


def prepare_kernel(size, queries, keys, values, qn_ref, kn_ref, vn_ref, buffer, sems, vsems):
    groups, _, width = queries.shape
    order = [(group, kind) for group in range(groups) for kind in (1, 0)]

    def fetch(step):
        group, kind = order[step]
        source = (queries, keys)[kind]
        return pltpu.make_async_copy(source.at[group], buffer.at[step % 3], sems.at[step % 3])

    def pull(group):
        return pltpu.make_async_copy(values.at[group], vn_ref.at[group], vsems.at[group])

    fetch(0).start()
    fetch(1).start()
    for step, (group, kind) in enumerate(order):
        if step + 2 < len(order):
            fetch(step + 2).start()
        if kind == 1:
            pull(group).start()
        fetch(step).wait()
        target = (qn_ref, kn_ref)[kind]
        for low in range(0, width, size):
            target[group, :, low : low + size] = rms_cast(buffer[step % 3, :, low : low + size])
    for group in range(groups):
        pull(group).wait()


def prepare(queries, keys, values, size):
    groups, rows, width = queries.shape
    return pl.pallas_call(
        functools.partial(prepare_kernel, size),
        in_specs=[OUTSIDE] * 3,
        out_specs=[WHOLE] * 3,
        out_shape=[pltpu.VMEM(queries.shape, BF16)] * 3,
        scratch_shapes=[
            pltpu.VMEM((3, rows, width), BF16),
            pltpu.SemaphoreType.DMA((3,)),
            pltpu.SemaphoreType.DMA((groups,)),
        ],
        compiler_params=params(8),
        name="prepare",
    )(queries, keys, values)


def join(core, own_ref, other_ref, full):
    half = own_ref.shape[1]
    mine = pl.multiple_of(core * half, half)
    theirs = pl.multiple_of((1 - core) * half, half)
    full[:, pl.ds(mine, half), :] = own_ref[...]
    full[:, pl.ds(theirs, half), :] = other_ref[...]
    return mine, theirs, half


def grads_kernel(
    group, head, core_ref, key_ref, value_ref, rate_ref, own_ref, other_ref,
    keep_ref, send_ref, full, sums,
):
    size = own_ref.shape[2]
    rows = key_ref.shape[1]
    mine, theirs, half = join(core_ref[0], own_ref, other_ref, full)
    columns = slice(head * size, (head + 1) * size)
    key_norm = key_ref[group, :, columns]
    value_now = value_ref[group, :, columns]
    rate = jnp.transpose(rate_ref[:, group * rows : (group + 1) * rows])
    gate = dot(key_norm, full[0], 1, 0)
    upper = dot(key_norm, full[1], 1, 0)
    back = dot(value_now, full[2], 1, 1)
    sig = jax.nn.sigmoid(gate)
    active = gate * sig
    hidden_key = (active * upper).astype(BF16)
    d_gate = back * upper * sig * (1.0 + gate * (1.0 - sig))
    d_up = back * active
    first = 3 * head
    err_gate = (rate[:, first : first + 1] * d_gate).astype(BF16)
    err_down = (rate[:, first + 1 : first + 2] * value_now.astype(F32)).astype(BF16)
    err_up = (rate[:, first + 2 : first + 3] * d_up).astype(BF16)
    sums[0] = dot(key_norm, err_gate, 0, 0)
    sums[1] = dot(key_norm, err_up, 0, 0)
    sums[2] = dot(hidden_key, err_down, 0, 0)
    keep_ref[...] = sums[:, pl.ds(mine, half), :]
    send_ref[...] = sums[:, pl.ds(theirs, half), :].astype(BF16)


def gradients(core, key_norm, values, rates, own, other, group, head):
    _, half, size = own.shape
    return pl.pallas_call(
        functools.partial(grads_kernel, group, head),
        in_specs=[SCALAR] + [WHOLE] * 5,
        out_specs=[WHOLE, WHOLE],
        out_shape=[pltpu.VMEM((3, half, size), F32), pltpu.VMEM((3, half, size), BF16)],
        scratch_shapes=[pltpu.VMEM((3, size, size), BF16), pltpu.VMEM((3, size, size), F32)],
        compiler_params=params(8),
        name="gradients",
    )(core, near(key_norm), near(values), near(rates), near(own), near(other))


def apply_kernel(group, head, core_ref, query_ref, own_ref, other_ref, *rest):
    out_ref, full = rest[-2:]
    size = own_ref.shape[2]
    join(core_ref[0], own_ref, other_ref, full)
    columns = slice(head * size, (head + 1) * size)
    query_norm = query_ref[group, :, columns]
    gate = dot(query_norm, full[0], 1, 0)
    upper = dot(query_norm, full[1], 1, 0)
    hidden_query = (gate * jax.nn.sigmoid(gate) * upper).astype(BF16)
    out_ref[group, :, columns] = dot(hidden_query, full[2], 1, 0).astype(BF16)


def apply_net(core, query_norm, own, other, out, group, head):
    size = own.shape[2]
    held = [] if out is None else [near(out)]
    return pl.pallas_call(
        functools.partial(apply_kernel, group, head),
        in_specs=[SCALAR] + [WHOLE] * (3 + len(held)),
        out_specs=WHOLE,
        out_shape=pltpu.VMEM(query_norm.shape, BF16),
        scratch_shapes=[pltpu.VMEM((3, size, size), BF16)],
        input_output_aliases={4: 0} if held else {},
        compiler_params=params(8),
        name="apply",
    )(core, near(query_norm), near(own), near(other), *held)


def both_cores(links):
    return [(2 * a + core, 2 * b + core) for a, b in links for core in (0, 1)]


def local(queries, keys, values, features, w_rate, fast_init, momentum):
    groups, rows, width = queries.shape
    heads, _, size, _ = fast_init.shape
    half = size // 2
    parts = lax.axis_size("head")
    count = lax.axis_size("ctx")
    nodes = count // 2
    levels = nodes // 2 - 1
    assert count == 2 * nodes and nodes == 2 * (levels + 1)
    place = lax.axis_index("ctx")
    core = (place % 2).astype(jnp.int32)
    node = place // 2
    depth = jnp.minimum(node, nodes - 1 - node)
    core_arg = core.reshape(1)

    pieces = partial_logits(features, w_rate, parts)
    seat = lax.axis_index("head")
    gathered = [lax.dynamic_index_in_dim(pieces, seat, 0, keepdims=False)]
    for step in range(1, parts):
        away = lax.dynamic_index_in_dim(pieces, (seat + step) % parts, 0, keepdims=False)
        gathered.append(
            lax.ppermute(away, "head", [(i, (i + step) % parts) for i in range(parts)])
        )
    rates = rates_of(gathered)
    query_norm, key_norm, value_now = prepare(queries, keys, values, size)

    def own_half(array, which):
        return lax.dynamic_slice_in_dim(array, which * half, half, 1)

    flips = [(i, i ^ 1) for i in range(count)]
    exchange = both_cores([(nodes // 2 - 1, nodes // 2), (nodes // 2, nodes // 2 - 1)])

    def level_pairs(level, inward, outward):
        links = []
        for near_end, far_end in ((level, level + 1), (nodes - 1 - level, nodes - 2 - level)):
            if inward:
                links.append((near_end, far_end))
            if outward:
                links.append((far_end, near_end))
        return both_cores(links)

    state, velocity, base, sent, other = [], [], [], {}, {}
    for head in range(heads):
        mine = own_half(fast_init[head], core)
        other[head] = own_half(fast_init[head], 1 - core)
        sent[head] = mine
        wide = mine.astype(F32)
        state.append(wide)
        base.append(jnp.sqrt(jnp.sum(wide * wide, axis=-1, keepdims=True)))
        velocity.append(jnp.zeros_like(wide))

    lap = max(heads, 2 * levels + 3)
    total = groups * heads

    def starting(tick):
        group, head = divmod(tick, lap)
        return group * heads + head if 0 <= group < groups and head < heads else None

    part = {}
    out = None
    tick = 0
    finished = 0
    while finished < total:
        for level in range(levels):
            inner, outer = starting(tick - 1 - level), starting(tick - 2 * levels - 2 + level)
            inward, outward = inner is not None, outer is not None
            if not (inward or outward):
                continue
            if inward and outward:
                load = jnp.where(depth == level, part[inner].astype(BF16), sent[outer])
            else:
                load = part[inner].astype(BF16) if inward else sent[outer]
            got = lax.ppermute(load, "ctx", level_pairs(level, inward, outward))
            if inward:
                part[inner] = part[inner] + jnp.where(depth == level + 1, got.astype(F32), 0.0)
            if outward:
                sent[outer] = jnp.where(depth == level, got, sent[outer])
        ready = starting(tick - 2 * levels - 3)
        if ready is not None:
            other[ready + heads] = lax.ppermute(sent[ready], "ctx", flips)
            sent[ready + heads] = sent[ready]
        new = starting(tick)
        if new is not None:
            group, head = divmod(new, heads)
            keep, send = gradients(
                core_arg, key_norm, value_now, rates, sent[new], other[new], group, head
            )
            part[new] = keep + lax.ppermute(send, "ctx", flips).astype(F32)
        if ready is not None:
            group, head = divmod(ready, heads)
            out = apply_net(
                core_arg, query_norm, sent[ready], other[ready + heads], out, group, head
            )
            finished += 1
        middle = starting(tick - 1 - levels)
        if middle is not None:
            head = middle % heads
            mine = part.pop(middle).astype(BF16)
            got = lax.ppermute(mine, "ctx", exchange)
            velocity[head] = (
                momentum[head] * velocity[head] + (mine.astype(F32) + got.astype(F32))
            )
            moved = state[head] + velocity[head]
            length = jnp.sqrt(jnp.sum(moved * moved, axis=-1, keepdims=True) + 1e-06)
            state[head] = moved * (base[head] / length)
            sent[middle] = state[head].astype(BF16)
        tick += 1
    return out


def solution(mesh):
    return jax.shard_map(
        local,
        mesh=mesh,
        in_specs=(
            P(None, "ctx", "head"),
            P(None, "ctx", "head"),
            P(None, "ctx", "head"),
            P(None, "ctx", "head"),
            P("head", None),
            P("head", None, None, None),
            P("head"),
        ),
        out_specs=P(None, "ctx", "head"),
        check_vma=False,
    )
```
